128 devices in a mesh: mem: 4 (over y), tok: 32 (over z, x, core).
Axes of the slice: x: 4, y: 4, z: 4, core: 2. Of those that a mesh axis runs over, the one named last changes fastest.
Arguments:
- queries: bfloat16 [32768, 4096], P('tok', 'mem'), may hold values from -6 to 6
- keys: bfloat16 [32768, 4096], P('tok', 'mem'), may hold values from -6 to 6
- values: bfloat16 [32768, 4096], P('tok', 'mem'), may hold values from -6 to 6
- memory: bfloat16 [32, 512, 128, 256], P('mem', 'tok'), may hold values from -6 to 6
- block_ids: int32 [64, 32, 4], P('tok', 'mem'), may hold values from 0 to 511, as said below
- gate_bias: float32 [32], P('mem'), may hold values from -2 to 2
- grad_out: bfloat16 [32768, 4096], P('tok', 'mem'), may hold values from -6 to 6
Outputs:
- output: bfloat16 [32768, 4096], P('tok', 'mem')
- grad_queries: bfloat16 [32768, 4096], P('tok', 'mem')
- grad_keys: bfloat16 [32768, 4096], P('tok', 'mem')
- grad_values: bfloat16 [32768, 4096], P('tok', 'mem')
The draws below stay inside these ranges and needn't reach their ends.
Inputs may be any that keep to these rules, and one draw needn't show every extreme that they name: `block_ids`: within one span and head the 4 ids differ. The ids held by one device (2 spans, 8 heads) name at most 4 blocks of any one memory shard (id // 16); in every draw some shard is named exactly 4 times by every such device.
All inputs are finite; a program needn't handle non-finite values.
Results may differ from the reference program's by a relative error of at most 0.02.
Values may be sent and summed in bfloat16 or wider, within the bound.
A program may use at most 128 MiB of HBM per device.

```python
import jax
import jax.numpy as jnp
from jax import lax

H = 32
HD = 128
SPAN_TOKENS = 512
BLOCK = 128
R = 4
SPAN_DEV = 2
NB_DEV = 16
HL = 8
CAP = 4
SPANS = 64
TOKENS = 32768
NB = 512


def token_field(key):
    shape = (TOKENS, H * HD)
    field = jnp.clip(jax.random.normal(key, shape, jnp.float32), -5.0, 5.0)
    return field.astype(jnp.bfloat16)


def draw_queries(key, part):
    return token_field(jax.random.fold_in(key, 31))


def draw_keys(key, part):
    inner = jax.random.fold_in(key, 32)
    return token_field(inner)


def draw_memory(key, part):
    inner = jax.random.fold_in(key, 33)
    field = jnp.clip(jax.random.normal(inner, (H, NB, BLOCK, 2 * HD), jnp.float32), -5.0, 5.0)
    return field.astype(jnp.bfloat16)


def draw_block_ids(key, part):
    tok_count = SPANS // SPAN_DEV
    mem_count = H // HL
    request_count = SPAN_DEV * HL * R
    slot_total = tok_count * CAP
    hot_owner = jax.random.randint(jax.random.fold_in(key, 11), (), 0, tok_count)
    slot_owner = jnp.arange(slot_total) // CAP

    def one_group(group_key):
        first_key, second_key, third_key = jax.random.split(group_key, 3)
        shuffled = slot_owner[jax.random.permutation(first_key, slot_total)]
        priority = jnp.where(shuffled == hot_owner, 0, 1 + jnp.arange(slot_total))
        chosen = shuffled[jnp.argsort(priority, stable=True)][:request_count]
        chosen = chosen[jax.random.permutation(second_key, request_count)]
        owners = chosen.reshape(SPAN_DEV * HL, R)
        same_owner = owners[:, :, None] == owners[:, None, :]
        rank_ids = jnp.arange(R)
        earlier = jnp.sum(same_owner & (rank_ids[None, None, :] < rank_ids[None, :, None]), axis=2)
        first_seen = jnp.min(jnp.where(same_owner, rank_ids[None, None, :], R), axis=2)
        offsets = jax.random.randint(third_key, (SPAN_DEV * HL, R), 0, NB_DEV)
        base_offset = jnp.take_along_axis(offsets, first_seen, axis=1)
        local_index = (base_offset + earlier) % NB_DEV
        return (owners * NB_DEV + local_index).reshape(SPAN_DEV, HL, R)
    group_keys = jax.random.split(jax.random.fold_in(key, 12), tok_count * mem_count)
    grouped = jax.vmap(one_group)(group_keys).reshape(tok_count, mem_count, SPAN_DEV, HL, R)
    return grouped.transpose(0, 2, 1, 3, 4).reshape(SPANS, H, R).astype(jnp.int32)


def block_levels(rng, dims, shards, least, largest):
    factor_of, own = 1.0, jax.random.fold_in(rng, 6)
    for axis_at, parts in shards:
        heights = jnp.exp(jax.random.uniform(jax.random.fold_in(own, axis_at), (parts,), jnp.float32, least / len(shards), largest / len(shards)))
        factor_of = factor_of * jnp.repeat(heights, dims[axis_at] // parts).reshape([-1 if axis == axis_at else 1 for axis in range(len(dims))])
    return factor_of


def gaussian(rng, dims, deviation, reach, pieces=(), held_as=jnp.bfloat16):
    values = jax.random.normal(rng, dims, jnp.float32) * deviation
    if len(pieces) > 0:
        values = block_levels(rng, dims, pieces, -0.22, 0.18) * values
    return jnp.clip(values, min=-reach, max=reach).astype(held_as)


def setup_inputs(seed: int = 0) -> dict:
    splits = jax.random.split(jax.random.key(seed), 8)
    queries = draw_queries(jax.random.fold_in(splits[7], 71), 0)
    keys = draw_keys(jax.random.fold_in(splits[7], 71), 0)
    values = gaussian(splits[2], (TOKENS, H * HD), 1.0, 6.0, ((0, 32), (1, 4)))
    memory = draw_memory(jax.random.fold_in(splits[7], 71), 0)
    block_ids = draw_block_ids(jax.random.fold_in(splits[7], 71), 0)
    gate_bias = jnp.clip(jax.random.uniform(splits[5], (H,), jnp.float32, -2.0, 2.0) * block_levels(splits[5], (H,), ((0, 4),), -0.4, 0.0), -2.0, 2.0)
    grad_out = gaussian(splits[6], (TOKENS, H * HD), 1.0, 6.0, ((0, 32), (1, 4)))
    return {"queries": queries, "keys": keys, "values": values, "memory": memory, "block_ids": block_ids, "gate_bias": gate_bias, "grad_out": grad_out}


def head_pass(query, keys_ext, values_ext, mem_keys, mem_values, grad_rows, gate_value, prev_ok):
    length = query.shape[0]
    scaling = query.shape[1] ** -0.5
    row_ids = jnp.arange(length)[:, None]
    col_ids = jnp.arange(2 * length)[None, :]
    allowed = (col_ids <= row_ids + length) & ((col_ids >= length) | prev_ok)
    scores = jnp.dot(query, keys_ext.T, preferred_element_type=jnp.float32) * scaling
    scores = jnp.where(allowed, scores, -jnp.inf)
    row_max = jnp.max(scores, axis=1, keepdims=True)
    weights = jnp.where(allowed, jnp.exp(scores - row_max), 0.0)
    row_sum = jnp.sum(weights, axis=1, keepdims=True)
    attention_weights = (weights / row_sum).astype(jnp.bfloat16)
    local_out = jnp.dot(attention_weights, values_ext, preferred_element_type=jnp.float32)
    mem_scores = jnp.dot(query, mem_keys.T, preferred_element_type=jnp.float32) * scaling
    mem_max = jnp.max(mem_scores, axis=1, keepdims=True)
    mem_weights = jnp.exp(mem_scores - mem_max)
    mem_probs = (mem_weights / jnp.sum(mem_weights, axis=1, keepdims=True)).astype(jnp.bfloat16)
    mem_out = jnp.dot(mem_probs, mem_values, preferred_element_type=jnp.float32)
    output = gate_value * mem_out + (1.0 - gate_value) * local_out
    grad_float = grad_rows.astype(jnp.float32)
    local_gradient = ((1.0 - gate_value) * grad_float).astype(jnp.bfloat16)
    grad_mem = (gate_value * grad_float).astype(jnp.bfloat16)
    local_dprobs = jnp.dot(local_gradient, values_ext.T, preferred_element_type=jnp.float32)
    extended_value_gradient = jnp.dot(attention_weights.T, local_gradient, preferred_element_type=jnp.float32)
    probs_float = attention_weights.astype(jnp.float32)
    row_dot = jnp.sum(probs_float * local_dprobs, axis=1, keepdims=True)
    local_dscores = (probs_float * (local_dprobs - row_dot) * scaling).astype(jnp.bfloat16)
    query_gradient = jnp.dot(local_dscores, keys_ext, preferred_element_type=jnp.float32)
    extended_key_gradient = jnp.dot(local_dscores.T, query, preferred_element_type=jnp.float32)
    mem_dprobs = jnp.dot(grad_mem, mem_values.T, preferred_element_type=jnp.float32)
    mem_float = mem_probs.astype(jnp.float32)
    mem_dot = jnp.sum(mem_float * mem_dprobs, axis=1, keepdims=True)
    mem_dscores = (mem_float * (mem_dprobs - mem_dot) * scaling).astype(jnp.bfloat16)
    query_gradient = query_gradient + jnp.dot(mem_dscores, mem_keys, preferred_element_type=jnp.float32)
    return (output.astype(jnp.bfloat16), query_gradient.astype(jnp.bfloat16), extended_key_gradient, extended_value_gradient,
            row_max[:, 0], row_sum[:, 0], row_dot[:, 0])


def span_sweep(query, keys_ext, values_ext, blocks, grad_rows, gates, prev_ok):
    head_count = gates.shape[0]
    head_size = blocks.shape[-1] // 2

    def split_heads(matrix):
        return matrix.reshape(matrix.shape[0], head_count, head_size).transpose(1, 0, 2)

    def join_heads(stacked):
        return stacked.transpose(1, 0, 2).reshape(stacked.shape[1], head_count * head_size)

    mem_keys = blocks[..., :head_size].reshape(head_count, -1, head_size)
    mem_values = blocks[..., head_size:].reshape(head_count, -1, head_size)

    def per_head(inputs):
        return head_pass(inputs[0], inputs[1], inputs[2], inputs[3], inputs[4], inputs[5], inputs[6], prev_ok)

    result = lax.map(per_head, (split_heads(query), split_heads(keys_ext), split_heads(values_ext),
                                mem_keys, mem_values, split_heads(grad_rows), gates))
    return (join_heads(result[0]), join_heads(result[1]), join_heads(result[2]), join_heads(result[3]),
            (result[4], result[5], result[6]))


def reference(queries, keys, values, memory, block_ids, gate_bias, grad_out):
    gates = jax.nn.sigmoid(gate_bias)
    width = H * HD
    zero_rows = jnp.zeros((SPAN_TOKENS, width), keys.dtype)
    keys_pad = jnp.concatenate([zero_rows, keys], axis=0)
    values_pad = jnp.concatenate([zero_rows, values], axis=0)
    head_rows = jnp.arange(H)[:, None]

    def step(running_state, index):
        start = (index * SPAN_TOKENS).astype(jnp.int32)
        query = lax.dynamic_slice_in_dim(queries, start, SPAN_TOKENS, 0)
        grad_rows = lax.dynamic_slice_in_dim(grad_out, start, SPAN_TOKENS, 0)
        keys_ext = lax.dynamic_slice_in_dim(keys_pad, start, 2 * SPAN_TOKENS, 0)
        values_ext = lax.dynamic_slice_in_dim(values_pad, start, 2 * SPAN_TOKENS, 0)
        picked = memory[head_rows, block_ids[index]]
        output, query_gradient, extended_key_gradient, extended_value_gradient, softmax_totals = span_sweep(
            query, keys_ext, values_ext, picked, grad_rows, gates, index > 0)
        key_gradient = (extended_key_gradient[SPAN_TOKENS:] + running_state[0]).astype(jnp.bfloat16)
        value_gradient = (extended_value_gradient[SPAN_TOKENS:] + running_state[1]).astype(jnp.bfloat16)
        return (extended_key_gradient[:SPAN_TOKENS], extended_value_gradient[:SPAN_TOKENS]), (output, query_gradient, key_gradient, value_gradient)

    start_carry = (jnp.zeros((SPAN_TOKENS, width), jnp.float32), jnp.zeros((SPAN_TOKENS, width), jnp.float32))
    final_carry, stacked = lax.scan(step, start_carry, jnp.arange(SPANS, dtype=jnp.int32), reverse=True)
    return (stacked[0].reshape(TOKENS, width), stacked[1].reshape(TOKENS, width),
            stacked[2].reshape(TOKENS, width), stacked[3].reshape(TOKENS, width))
```

```python
import functools
import math

import jax
import jax.numpy as jnp
from jax import lax
from jax.experimental import pallas as pl
from jax.experimental.pallas import tpu as pltpu
from jax.sharding import PartitionSpec as P

SPAN_TOKENS = 512
BLOCK = 128
R = 4
HD = 128
CHUNK = 256
SCALE = HD ** -0.5
EXP_SCALE = SCALE / math.log(2.0)
NEG = -1e30
F32 = jnp.float32
BF16 = jnp.bfloat16


def dot_nn(a, b):
    return lax.dot_general(a, b, (((1,), (0,)), ((), ())), preferred_element_type=F32)


def dot_nt(a, b):
    return lax.dot_general(a, b, (((1,), (1,)), ((), ())), preferred_element_type=F32)


def passed_along(block, axis, distance):
    devices = range(lax.axis_size(axis))
    route = [(i - distance, i) for i in devices if i - distance in devices]
    return lax.ppermute(block, axis, route)


def gather_kernel(codes, *refs):
    blocks, out = refs[:-1], refs[-1]
    for i, block in enumerate(blocks):
        out[i] = block[0]


def gather_blocks(memory, codes, per_step=16):
    count = codes.shape[0]
    width = memory.shape[-1]

    def spec(i):
        return pl.BlockSpec((1, BLOCK, width), lambda s, c: (c[s * per_step + i], 0, 0))

    return pl.pallas_call(
        gather_kernel,
        out_shape=jax.ShapeDtypeStruct((count, BLOCK, width), memory.dtype),
        grid_spec=pltpu.PrefetchScalarGridSpec(
            num_scalar_prefetch=1,
            grid=(count // per_step,),
            in_specs=[spec(i) for i in range(per_step)],
            out_specs=pl.BlockSpec((per_step, BLOCK, width), lambda s, c: (s, 0, 0)),
        ),
        name="gather_blocks",
    )(codes, *([memory] * per_step))


def softmax_part(pieces, biases):
    top = None
    for piece, bias in zip(pieces, biases):
        piece_top = jnp.max(piece, axis=0, keepdims=True)
        if bias is not None:
            piece_top = piece_top + bias
        top = piece_top if top is None else jnp.maximum(top, piece_top)
    total, weights = None, []
    for piece, bias in zip(pieces, biases):
        shift = top if bias is None else top - bias
        weight = jnp.exp2((piece - shift) * EXP_SCALE)
        part = jnp.sum(weight, axis=0, keepdims=True)
        total = part if total is None else total + part
        weights.append(weight.astype(BF16))
    return weights, total


def local_kernel(add_prev, gate_ref, flag_ref, q_ref, g_ref, kp_ref, vp_ref, kc_ref, vc_ref, *refs):
    if add_prev:
        ak_ref, av_ref = refs[:2]
        refs = refs[2:]
    out_ref, dq_ref, dkp_ref, dvp_ref, dkc_ref, dvc_ref, kacc, vacc = refs
    head = pl.program_id(0)
    gate = gate_ref[head]
    bias = jnp.where(flag_ref[0] > 0, 0.0, NEG).astype(F32)
    length = SPAN_TOKENS
    keys = (kp_ref[...], kc_ref[...])
    values = (vp_ref[...], vc_ref[...])
    keys_t = [k.T for k in keys]
    values_t = [v.T for v in values]
    for chunk in range(length // CHUNK):
        rows = slice(chunk * CHUNK, (chunk + 1) * CHUNK)
        q = q_ref[rows, :]
        q_t = q.T
        g_t = g_ref[rows, :].astype(F32).T
        spans = [(0, 0, length)]
        if chunk:
            spans.append((1, 0, chunk * CHUNK))
        spans.append((1, chunk * CHUNK, CHUNK))
        pieces = [dot_nn(keys[w][a : a + n], q_t) for w, a, n in spans]
        col = lax.broadcasted_iota(jnp.int32, (CHUNK, CHUNK), 0)
        row = lax.broadcasted_iota(jnp.int32, (CHUNK, CHUNK), 1)
        pieces[-1] = jnp.where(col <= row, pieces[-1], NEG)
        biases = [bias] + [None] * (len(spans) - 1)
        weights, total = softmax_part(pieces, biases)
        inverse = 1.0 / total
        out_t = sum(dot_nn(values_t[w][:, a : a + n], e) for (w, a, n), e in zip(spans, weights))
        out_t = out_t * inverse
        grad_t = (g_t * ((1.0 - gate) * inverse)).astype(BF16)
        grad = grad_t.T
        row_dot = jnp.sum(grad_t.astype(F32) * out_t, axis=0, keepdims=True)
        dq_t = None
        for (w, a, n), e in zip(spans, weights):
            dprobs = dot_nn(values[w][a : a + n], grad_t)
            dscores = e * (dprobs - row_dot).astype(BF16)
            part = dot_nn(keys_t[w][:, a : a + n], dscores)
            dq_t = part if dq_t is None else dq_t + part
            dk = dot_nn(dscores, q)
            dv = dot_nn(e, grad)
            at = pl.ds(w * length + a, n)
            if chunk == 0 or (w == 1 and a == chunk * CHUNK):
                kacc[at, :] = dk
                vacc[at, :] = dv
            else:
                kacc[at, :] += dk
                vacc[at, :] += dv
        out_ref[rows, :] = (out_t * (1.0 - gate)).T.astype(out_ref.dtype)
        dq_ref[rows, :] = (dq_t * SCALE).T.astype(dq_ref.dtype)
    dkp_ref[...] = (kacc[:length, :] * SCALE).astype(dkp_ref.dtype)
    dvp_ref[...] = vacc[:length, :].astype(dvp_ref.dtype)
    dkc, dvc = kacc[length:, :] * SCALE, vacc[length:, :]
    if add_prev:
        dkc = dkc + ak_ref[...]
        dvc = dvc + av_ref[...]
    dkc_ref[...] = dkc.astype(dkc_ref.dtype)
    dvc_ref[...] = dvc.astype(dvc_ref.dtype)


def local_part(gates, flag, queries, grads, span, kp, vp, kc, vc, added, prev_type):
    heads = gates.shape[0]

    def spec(index):
        return pl.BlockSpec((SPAN_TOKENS, HD), lambda h: (index, h))

    smem = pl.BlockSpec(memory_space=pltpu.SMEM)
    operands = [gates, flag, queries, grads, kp[0], vp[0], kc[0], vc[0]]
    specs = [smem, smem, spec(span), spec(span)] + [spec(x[1]) for x in (kp, vp, kc, vc)]
    if added is not None:
        operands += list(added)
        specs += [spec(0), spec(0)]
    shape = (SPAN_TOKENS, heads * HD)
    types = [BF16, BF16, prev_type, prev_type, BF16, BF16]
    return pl.pallas_call(
        functools.partial(local_kernel, added is not None),
        grid=(heads,),
        out_shape=[jax.ShapeDtypeStruct(shape, t) for t in types],
        in_specs=specs,
        out_specs=[spec(0)] * 6,
        scratch_shapes=[pltpu.VMEM((2 * SPAN_TOKENS, HD), F32)] * 2,
        cost_estimate=pl.CostEstimate(
            flops=heads * 6 * 2 * SPAN_TOKENS * 2 * SPAN_TOKENS * HD,
            bytes_accessed=heads * SPAN_TOKENS * HD * 2 * 12,
            transcendentals=heads * SPAN_TOKENS * 2 * SPAN_TOKENS,
        ),
        name="local_part_%d" % span,
    )(*operands)


def memory_kernel(slots, gate_ref, q_ref, g_ref, o0, o1, d0, d1, k0, k1, kl, v0, v1, vl, *refs):
    blocks, (out_ref, dq_ref, dk_ref, dv_ref) = refs[:-4], refs[-4:]
    gate = gate_ref[pl.program_id(0)]
    length = SPAN_TOKENS
    for span, (o_in, d_in) in enumerate(((o0, d0), (o1, d1))):
        mine = [b[0] for b in blocks[span * R : (span + 1) * R]]
        keys = jnp.concatenate([b[:, :HD] for b in mine], axis=0)
        values = jnp.concatenate([b[:, HD:] for b in mine], axis=0)
        keys_t, values_t = keys.T, values.T
        for chunk in range(length // CHUNK):
            here = slice(chunk * CHUNK, (chunk + 1) * CHUNK)
            rows = slice(span * length + chunk * CHUNK, span * length + (chunk + 1) * CHUNK)
            q_t = q_ref[rows, :].T
            g_t = g_ref[rows, :].astype(F32).T
            (e,), total = softmax_part([dot_nn(keys, q_t)], [None])
            inverse = 1.0 / total
            out_t = dot_nn(values_t, e) * inverse
            grad_t = (g_t * (gate * inverse)).astype(BF16)
            row_dot = jnp.sum(grad_t.astype(F32) * out_t, axis=0, keepdims=True)
            dscores = e * (dot_nn(values, grad_t) - row_dot).astype(BF16)
            dq_t = dot_nn(keys_t, dscores)
            out_ref[rows, :] = ((out_t * gate).T + o_in[here, :].astype(F32)).astype(out_ref.dtype)
            dq_ref[rows, :] = ((dq_t * SCALE).T + d_in[here, :].astype(F32)).astype(dq_ref.dtype)
    dk_ref[:length, :] = k0[...]
    dv_ref[:length, :] = v0[...]
    dk_ref[length:, :] = (k1[...].astype(F32) + kl[...].astype(F32)).astype(dk_ref.dtype)
    dv_ref[length:, :] = (v1[...].astype(F32) + vl[...].astype(F32)).astype(dv_ref.dtype)


def memory_part(gates, slots, queries, grads, returned, outs, dqs, dks, dvs):
    heads = gates.shape[0]
    tokens, width = queries.shape
    half = pl.BlockSpec((SPAN_TOKENS, HD), lambda h, s: (0, h))
    full = pl.BlockSpec((tokens, HD), lambda h, s: (0, h))
    spans = tokens // SPAN_TOKENS

    def lead_spec(index):
        return pl.BlockSpec((SPAN_TOKENS, HD), lambda h, s: (index, h))

    def block_spec(span, r):
        return pl.BlockSpec(
            (1, BLOCK, 2 * HD), lambda h, s: (s[(span * heads + h) * R + r], 0, 0)
        )

    picked = [block_spec(span, r) for span in range(spans) for r in range(R)]
    shape = jax.ShapeDtypeStruct((tokens, width), BF16)
    return pl.pallas_call(
        memory_kernel,
        out_shape=[shape] * 4,
        grid_spec=pltpu.PrefetchScalarGridSpec(
            num_scalar_prefetch=1,
            grid=(heads,),
            in_specs=[pl.BlockSpec(memory_space=pltpu.SMEM), full, full]
            + [half] * 6 + [lead_spec(0)] + [half] * 2 + [lead_spec(1)] + picked,
            out_specs=[full] * 4,
        ),
        name="memory_part",
    )(slots, gates, queries, grads, *outs, *dqs, *dks, *dvs, *([returned] * len(picked)))


def per_device(queries, keys, values, memory, block_ids, gate_bias, grad_out):
    tok_count = lax.axis_size("tok")
    my_rank = lax.axis_index("tok")
    heads_here = gate_bias.shape[0]
    gates = jax.nn.sigmoid(gate_bias)
    tail_rows = jnp.concatenate([keys[-SPAN_TOKENS:], values[-SPAN_TOKENS:]], axis=0)
    before = passed_along(tail_rows, "tok", 1)
    blocks_here = memory.shape[1]
    wanted = block_ids.reshape(-1)
    request_count = wanted.shape[0]
    owner_rank = wanted // blocks_here
    head_index = jnp.arange(request_count) // R % heads_here
    request_code = head_index * blocks_here + wanted % blocks_here
    order_ids = jnp.arange(request_count)
    same_owner = owner_rank[:, None] == owner_rank[None, :]
    slot_index = jnp.sum(same_owner & (order_ids[None, :] < order_ids[:, None]), axis=1)
    capacity = 2 * request_count // tok_count
    to_owner = (owner_rank[:, None] == jnp.arange(tok_count)[None, :]).astype(jnp.int32)
    to_slot = (slot_index[:, None] == jnp.arange(capacity)[None, :]).astype(jnp.int32)
    request_table = jnp.sum(
        request_code[:, None, None] * to_owner[:, :, None] * to_slot[:, None, :], axis=0
    )
    asked = lax.all_to_all(request_table, "tok", split_axis=0, concat_axis=0, tiled=True)
    mem_flat = memory.reshape(-1, BLOCK, memory.shape[-1])
    found = gather_blocks(mem_flat, asked.reshape(-1))
    returned = lax.all_to_all(found, "tok", split_axis=0, concat_axis=0, tiled=True)
    slots = (owner_rank * capacity + slot_index).astype(jnp.int32)

    yes = jnp.ones((1,), jnp.int32)
    out1, dq1, ak, av, dk1, dv1 = local_part(
        gates, yes, queries, grad_out, 1, (keys, 0), (values, 0), (keys, 1), (values, 1), None, F32
    )
    not_first = (my_rank > 0).astype(jnp.int32).reshape(1)
    out0, dq0, lead_k, lead_v, dk0, dv0 = local_part(
        gates, not_first, queries, grad_out, 0, (before, 0), (before, 1), (keys, 0), (values, 0), (ak, av), BF16
    )
    incoming = passed_along(jnp.concatenate([lead_k, lead_v], axis=0), "tok", -1)
    return tuple(memory_part(
        gates, slots, queries, grad_out, returned,
        (out0, out1), (dq0, dq1), (dk0, dk1, incoming), (dv0, dv1, incoming),
    ))


def solution(mesh):
    in_specs = (
        P("tok", "mem"),
        P("tok", "mem"),
        P("tok", "mem"),
        P("mem", "tok", None, None),
        P("tok", "mem", None),
        P("mem"),
        P("tok", "mem"),
    )
    out_specs = (P("tok", "mem"), P("tok", "mem"), P("tok", "mem"), P("tok", "mem"))
    return jax.shard_map(
        per_device, mesh=mesh, in_specs=in_specs, out_specs=out_specs, check_vma=False
    )
```

```python
import math
import random

import jax
import jax.numpy as jnp
from jax import lax
from jax.experimental import pallas as pl
from jax.experimental.pallas import tpu as pltpu
from jax.sharding import PartitionSpec as P

SPAN = 512
BLOCK = 128
R = 4
HD = 128
CHUNK = 256
SCALE = HD ** -0.5
EXP_SCALE = SCALE / math.log(2.0)
NEG = -1e30
F32 = jnp.float32
BF16 = jnp.bfloat16
MESH = pl.DeviceIdType.MESH


def dot_nn(a, b):
    return lax.dot_general(a, b, (((1,), (0,)), ((), ())), preferred_element_type=F32)


def softmax_part(pieces, biases):
    top = None
    for piece, bias in zip(pieces, biases):
        piece_top = jnp.max(piece, axis=0, keepdims=True)
        if bias is not None:
            piece_top = piece_top + bias
        top = piece_top if top is None else jnp.maximum(top, piece_top)
    total, weights = None, []
    for piece, bias in zip(pieces, biases):
        shift = top if bias is None else top - bias
        weight = jnp.exp2((piece - shift) * EXP_SCALE)
        part = jnp.sum(weight, axis=0, keepdims=True)
        total = part if total is None else total + part
        weights.append(weight.astype(BF16))
    return weights, total


def cols(h):
    return pl.ds(pl.multiple_of(h * HD, HD), HD)


def window_pass(span, h, gate, bias, q_ref, g_ref, keys, values, out_ref, dq_ref, kacc, vacc):
    keys_t = [k.T for k in keys]
    values_t = [v.T for v in values]
    for chunk in range(SPAN // CHUNK):
        rows = pl.ds(span * SPAN + chunk * CHUNK, CHUNK)
        q = q_ref[rows, cols(h)]
        q_t = q.T
        g_t = g_ref[rows, cols(h)].astype(F32).T
        parts = [(0, 0, SPAN)]
        if chunk:
            parts.append((1, 0, chunk * CHUNK))
        parts.append((1, chunk * CHUNK, CHUNK))
        pieces = [dot_nn(keys[w][a : a + n], q_t) for w, a, n in parts]
        col = lax.broadcasted_iota(jnp.int32, (CHUNK, CHUNK), 0)
        row = lax.broadcasted_iota(jnp.int32, (CHUNK, CHUNK), 1)
        pieces[-1] = jnp.where(col <= row, pieces[-1], NEG)
        weights, total = softmax_part(pieces, [bias] + [None] * (len(parts) - 1))
        inverse = 1.0 / total
        out_t = sum(dot_nn(values_t[w][:, a : a + n], e) for (w, a, n), e in zip(parts, weights))
        out_t = out_t * inverse
        grad_t = (g_t * ((1.0 - gate) * inverse)).astype(BF16)
        grad = grad_t.T
        row_dot = jnp.sum(grad_t.astype(F32) * out_t, axis=0, keepdims=True)
        dq_t = None
        for (w, a, n), e in zip(parts, weights):
            dprobs = dot_nn(values[w][a : a + n], grad_t)
            dscores = e * (dprobs - row_dot).astype(BF16)
            part = dot_nn(keys_t[w][:, a : a + n], dscores)
            dq_t = part if dq_t is None else dq_t + part
            dk = dot_nn(dscores, q)
            dv = dot_nn(e, grad)
            at = pl.ds(w * SPAN + a, n)
            if chunk == 0 or (w == 1 and a == chunk * CHUNK):
                kacc[at, :] = dk
                vacc[at, :] = dv
            else:
                kacc[at, :] += dk
                vacc[at, :] += dv
        out_ref[rows, cols(h)] = (out_t * (1.0 - gate)).T.astype(BF16)
        dq_ref[rows, cols(h)] = (dq_t * SCALE).T.astype(BF16)


def body(order, heads, gate_ref, slot_ref, codes_ref, q_hbm, k_hbm, v_hbm, g_hbm, mem_hbm,
         out_hbm, dq_hbm, dk_hbm, dv_hbm,
         q_ref, k_ref, v_ref, g_ref, mem, stage, recv_k, recv_v, tails, lead_out, lead_in,
         out_ref, dq_ref, dk_ref, dv_ref, grads, sums, kacc, vacc, codes, codes_s,
         in_sem, code_send, code_recv, tail_send, tail_recv, send_sem, recv_sem, lead_send, lead_recv, out_sem):
    me = lax.axis_index("tok")
    count = lax.axis_size("tok")
    capacity = stage.shape[1]

    loads = [pltpu.make_async_copy(src, dst, in_sem.at[i]) for i, (src, dst) in enumerate((
        (mem_hbm, mem), (q_hbm, q_ref), (k_hbm, k_ref), (v_hbm, v_ref), (g_hbm, g_ref)))]
    for load in loads:
        load.start()

    def peer(offset):
        return lax.rem(me + offset, count)

    barrier = pltpu.get_barrier_semaphore()
    for offset in order:
        pl.semaphore_signal(barrier, inc=1, device_id={"tok": peer(offset)}, device_id_type=MESH)
    pl.semaphore_wait(barrier, len(order))

    def remote(src, dst, send, recv, offset):
        return pltpu.make_async_remote_copy(
            src_ref=src, dst_ref=dst, send_sem=send, recv_sem=recv,
            device_id={"tok": peer(offset)}, device_id_type=MESH)

    asks = [remote(codes_ref.at[peer(o)], codes.at[me], code_send.at[i], code_recv.at[i], o)
            for i, o in enumerate(order)]
    for ask in asks:
        ask.start()
    own = pl.ds(SPAN, SPAN)
    tail_copies = [remote(src.at[own], tails.at[i], tail_send.at[i], tail_recv.at[i], 1)
                   for i, src in enumerate((k_hbm, v_hbm))]
    for copy in tail_copies:
        copy.start()
    codes[me] = codes_ref[me]
    for ask in asks:
        ask.wait()
    to_scalars = pltpu.make_async_copy(codes, codes_s, in_sem.at[5])
    to_scalars.start()
    loads[0].wait()
    to_scalars.wait()

    recvs = (recv_k, recv_v)

    def block_copy(kind, s, i, o):
        return remote(stage.at[kind, s, peer(o)], recvs[kind].at[me * capacity + s],
                      send_sem.at[kind, s, i], recv_sem.at[kind, s, i], o)

    for kind in range(2):
        half = slice(kind * HD, (kind + 1) * HD)

        def fill(s, carry):
            for o in order:
                to = peer(o)
                stage[kind, s, to] = mem[codes_s[to, 0, s], :, half]
            recvs[kind][me * capacity + s] = mem[codes_s[me, 0, s], :, half]
            return carry

        def send(s, carry):
            for i, o in enumerate(order):
                block_copy(kind, s, i, o).start()
            return carry

        lax.fori_loop(0, capacity, fill, 0)
        lax.fori_loop(0, capacity, send, 0)

    for load in loads[1:]:
        load.wait()

    first, second = slice(0, SPAN), slice(SPAN, 2 * SPAN)

    def late_span(h, carry):
        keys = (k_ref[first, cols(h)], k_ref[second, cols(h)])
        values = (v_ref[first, cols(h)], v_ref[second, cols(h)])
        window_pass(1, h, gate_ref[h], None, q_ref, g_ref, keys, values, out_ref, dq_ref, kacc, vacc)
        dk_ref[:, cols(h)] = (kacc[...] * SCALE).astype(BF16)
        dv_ref[:, cols(h)] = vacc[...].astype(BF16)
        return carry

    lax.fori_loop(0, heads, late_span, 0)
    for copy in tail_copies:
        copy.wait()

    bias = jnp.where(me > 0, 0.0, NEG).astype(F32)

    def lead_copy(h):
        return remote(lead_out.at[h], lead_in.at[h], lead_send.at[h], lead_recv.at[h], count - 1)

    def early_span(h, carry):
        keys = (tails[0, :, cols(h)], k_ref[first, cols(h)])
        values = (tails[1, :, cols(h)], v_ref[first, cols(h)])
        window_pass(0, h, gate_ref[h], bias, q_ref, g_ref, keys, values, out_ref, dq_ref, kacc, vacc)
        lead_out[h, 0] = (kacc[first, :] * SCALE).astype(BF16)
        lead_out[h, 1] = vacc[first, :].astype(BF16)
        dk_ref[first, cols(h)] = (kacc[second, :] * SCALE + dk_ref[first, cols(h)].astype(F32)).astype(BF16)
        dv_ref[first, cols(h)] = (vacc[second, :] + dv_ref[first, cols(h)].astype(F32)).astype(BF16)

        @pl.when(h > 0)
        def _():
            lead_copy(h - 1).start()

        return carry

    lax.fori_loop(0, heads, early_span, 0)

    def wait_blocks(kind):
        def step(s, carry):
            for i, o in enumerate(order):
                block_copy(kind, s, i, o).wait_recv()
            return carry

        lax.fori_loop(0, capacity, step, 0)

    wait_blocks(0)
    lead_copy(heads - 1).start()

    chunks = SPAN // CHUNK

    def picked(ref, span, h):
        return [ref[slot_ref[(span * heads + h) * R + r]] for r in range(R)]

    def key_step(unit, carry):
        span, h = unit // heads, unit % heads
        keys = jnp.concatenate(picked(recv_k, span, h), axis=0)
        for chunk in range(chunks):
            rows = pl.ds(pl.multiple_of(span * SPAN + chunk * CHUNK, CHUNK), CHUNK)
            at = unit * chunks + chunk
            q_t = q_ref[rows, cols(h)].T
            g_t = g_ref[rows, cols(h)].astype(F32).T
            (e,), total = softmax_part([dot_nn(keys, q_t)], [None])
            inverse = 1.0 / total
            for r in range(R):
                mem[at * R + r] = e[r * BLOCK : (r + 1) * BLOCK]
            grads[at] = (g_t * (gate_ref[h] * inverse)).astype(BF16)
            sums[at] = inverse
        return carry

    lax.fori_loop(0, 2 * heads, key_step, 0)
    wait_blocks(1)

    def value_step(h, carry):
        gate = gate_ref[h]
        for span in range(2):
            keys_t = jnp.concatenate([b.T for b in picked(recv_k, span, h)], axis=1)
            blocks = picked(recv_v, span, h)
            values = jnp.concatenate(blocks, axis=0)
            values_t = jnp.concatenate([b.T for b in blocks], axis=1)
            for chunk in range(chunks):
                rows = pl.ds(span * SPAN + chunk * CHUNK, CHUNK)
                at = (span * heads + h) * chunks + chunk
                e = jnp.concatenate([mem[at * R + r] for r in range(R)], axis=0)
                grad_t = grads[at]
                out_t = dot_nn(values_t, e) * sums[at]
                row_dot = jnp.sum(grad_t.astype(F32) * out_t, axis=0, keepdims=True)
                dscores = e * (dot_nn(values, grad_t) - row_dot).astype(BF16)
                dq_t = dot_nn(keys_t, dscores)
                out_ref[rows, cols(h)] = ((out_t * gate).T + out_ref[rows, cols(h)].astype(F32)).astype(BF16)
                dq_ref[rows, cols(h)] = ((dq_t * SCALE).T + dq_ref[rows, cols(h)].astype(F32)).astype(BF16)
        lead_copy(h).wait_recv()
        dk_ref[second, cols(h)] = (dk_ref[second, cols(h)].astype(F32) + lead_in[h, 0].astype(F32)).astype(BF16)
        dv_ref[second, cols(h)] = (dv_ref[second, cols(h)].astype(F32) + lead_in[h, 1].astype(F32)).astype(BF16)

        @pl.when(h > 0)
        def _():
            for i in range(4):
                store(h - 1, i).start()

        return carry

    targets = ((out_ref, out_hbm), (dq_ref, dq_hbm), (dk_ref, dk_hbm), (dv_ref, dv_hbm))

    def store(h, i):
        src, dst = targets[i]
        return pltpu.make_async_copy(src.at[:, cols(h)], dst.at[:, cols(h)], out_sem.at[i, h])

    lax.fori_loop(0, heads, value_step, 0)
    for i in range(4):
        store(heads - 1, i).start()

    def drain(s, carry):
        for kind in range(2):
            for i, o in enumerate(order):
                block_copy(kind, s, i, o).wait_send()
        return carry

    lax.fori_loop(0, capacity, drain, 0)

    def finish(h, carry):
        lead_copy(h).wait_send()
        for i in range(4):
            store(h, i).wait()
        return carry

    lax.fori_loop(0, heads, finish, 0)


def fused(capacity, order, gates, slots, codes, queries, keys, values, grad_out, memory):
    tokens, width = queries.shape
    heads = gates.shape[0]
    count = codes.shape[0]

    peers = len(order)
    units = 2 * heads * (SPAN // CHUNK)
    anywhere = pl.BlockSpec(memory_space=pl.ANY)
    smem = pl.BlockSpec(memory_space=pltpu.SMEM)
    vmem = pl.BlockSpec(memory_space=pltpu.VMEM)
    shape = jax.ShapeDtypeStruct((tokens, width), BF16)
    whole = pltpu.VMEM((tokens, width), BF16)
    dma = pltpu.SemaphoreType.DMA
    scratch = [whole] * 4 + [
        pltpu.VMEM(memory.shape, BF16),
        pltpu.VMEM((2, capacity, count, BLOCK, HD), BF16),
        pltpu.VMEM((count * capacity, BLOCK, HD), BF16),
        pltpu.VMEM((count * capacity, BLOCK, HD), BF16),
        pltpu.VMEM((2, SPAN, width), BF16),
        pltpu.VMEM((heads, 2, SPAN, HD), BF16),
        pltpu.VMEM((heads, 2, SPAN, HD), BF16),
    ] + [whole] * 4 + [
        pltpu.VMEM((units, HD, CHUNK), BF16),
        pltpu.VMEM((units, 1, CHUNK), F32),
        pltpu.VMEM((2 * SPAN, HD), F32),
        pltpu.VMEM((2 * SPAN, HD), F32),
        pltpu.VMEM(codes.shape, jnp.int32),
        pltpu.SMEM(codes.shape, jnp.int32),
        dma((6,)), dma((peers,)), dma((peers,)), dma((2,)), dma((2,)),
        dma((2, capacity, peers)), dma((2, capacity, peers)), dma((heads,)), dma((heads,)), dma((4, heads)),
    ]

    def kernel(*refs):
        body(order, heads, *refs)

    return pl.pallas_call(
        kernel,
        out_shape=[shape] * 4,
        in_specs=[smem, smem, vmem] + [anywhere] * 5,
        out_specs=[anywhere] * 4,
        scratch_shapes=scratch,
        compiler_params=pltpu.CompilerParams(
            collective_id=0, has_side_effects=True, vmem_limit_bytes=63 * 1024 * 1024),
        name="fused_step",
    )(gates, slots, codes, queries, keys, values, grad_out, memory)


def peer_order(count):
    order = list(range(1, count))
    random.Random(1).shuffle(order)
    return order


def per_device(queries, keys, values, memory, block_ids, gate_bias, grad_out):
    tok_count = lax.axis_size("tok")
    heads_here = gate_bias.shape[0]
    gates = jax.nn.sigmoid(gate_bias)
    blocks_here = memory.shape[1]
    wanted = block_ids.reshape(-1)
    request_count = wanted.shape[0]
    owner_rank = wanted // blocks_here
    head_index = jnp.arange(request_count) // R % heads_here
    request_code = head_index * blocks_here + wanted % blocks_here
    order_ids = jnp.arange(request_count)
    same_owner = owner_rank[:, None] == owner_rank[None, :]
    slot_index = jnp.sum(same_owner & (order_ids[None, :] < order_ids[:, None]), axis=1)
    capacity = 2 * request_count // tok_count
    to_owner = (owner_rank[:, None] == jnp.arange(tok_count)[None, :]).astype(jnp.int32)
    to_slot = (slot_index[:, None] == jnp.arange(128)[None, :]).astype(jnp.int32)
    codes = jnp.sum(request_code[:, None, None] * to_owner[:, :, None] * to_slot[:, None, :], axis=0)
    slots = (owner_rank * capacity + slot_index).astype(jnp.int32)
    return tuple(fused(
        capacity, peer_order(tok_count), gates, slots, codes[:, None, :].astype(jnp.int32), queries, keys, values, grad_out,
        memory.reshape(-1, BLOCK, memory.shape[-1])))


def solution(mesh):
    in_specs = (
        P("tok", "mem"),
        P("tok", "mem"),
        P("tok", "mem"),
        P("mem", "tok", None, None),
        P("tok", "mem", None),
        P("mem"),
        P("tok", "mem"),
    )
    out_specs = (P("tok", "mem"), P("tok", "mem"), P("tok", "mem"), P("tok", "mem"))
    return jax.shard_map(
        per_device, mesh=mesh, in_specs=in_specs, out_specs=out_specs, check_vma=False
    )
```
